32 devices in a mesh: groups: 2 (over x), img: 16 (over z, y, core).
Axes of the slice: x: 2, y: 2, z: 4, core: 2. Of those that a mesh axis runs over, the one named last changes fastest.
Arguments:
- descriptors: bfloat16 [64, 384, 256], P(('groups', 'img')), parts along dimension 0, may hold values from -6 to 6
- pair_list: int32 [128, 2], P(('groups', 'img')), parts along dimension 0, may hold values from -1 to 31, as said below
- key_proj: bfloat16 [256, 256], replicated, may hold values from -0.375 to 0.375
- value_proj: bfloat16 [256, 256], replicated, may hold values from -0.375 to 0.375
- out_proj: bfloat16 [256, 256], replicated, may hold values from -0.375 to 0.375
- ffn_first: bfloat16 [512, 512], replicated, may hold values from -0.25 to 0.25
- norm_gain: float32 [512], replicated, may hold values from 0.5 to 1.5
- norm_bias: float32 [512], replicated, may hold values from -3 to 3
- ffn_second: bfloat16 [512, 256], replicated, may hold values from -0.25 to 0.25
Outputs:
- updated: bfloat16 [64, 384, 256], P(('groups', 'img')), parts along dimension 0
The draws below stay inside these ranges and needn't reach their ends.
There are 2 independent parts, one for each index of `groups`. The reference program is written for one: setup_inputs(seed, part) draws one part's arguments, and reference() takes and returns one part's arrays. A program takes and returns all parts, laid end to end along the dimension named above; an argument that names none is the same for every part. Nothing has to cross between parts.
Inputs may be any that keep to these rules, and one draw needn't show every extreme that they name: `pair_list`: rows come in groups of 4, group g on index g of img. In each group the used rows come first, 2 to 4 of them; unused rows hold -1 in both columns. A used row (i, j) has i in images 2 * g to 2 * (g + 1) - 1, j different from i and in images 2 * g to 2 * (g + 3) - 1. Slot s below 2 of group g has i = 2 * g + s. Some group uses all 4 rows and has a second image in group g + 2.
All inputs are finite; a program needn't handle non-finite values.
Results may differ from the reference program's by a relative error of at most 0.0052.
Values may be sent and summed in bfloat16 or wider, within the bound.
No kernel may reach another device: no remote copies, remote signals or barrier semaphores. Data moves between devices by JAX's collectives and lax.ppermute only.
A program may use at most 128 MiB of HBM per device.

```python
import math
import jax
import jax.numpy as jnp
from jax import lax

D = 256
HEADS = 4
HID = 512
KEYPTS = 384
IMG_DEV = 2
PAIR_CAP = 4
REACH = 2
IMG = 32
PAIRS = 64


def draw_descriptors(key, part):
    noise_key = jax.random.fold_in(key, 0)
    full_shape = (IMG, KEYPTS, D)
    values = jnp.clip(jax.random.normal(noise_key, full_shape), -6.0, 6.0)
    return values.astype(jnp.bfloat16)


def draw_pair_list(key, part):
    group_count = PAIRS // PAIR_CAP
    split_keys = jax.random.split(key, 5)
    groups = jnp.arange(group_count)
    slot_ids = jnp.arange(PAIR_CAP)
    used = jax.random.randint(split_keys[0], (group_count,), IMG_DEV, PAIR_CAP + 1)
    busiest = jax.random.randint(split_keys[1], (), 0, group_count - REACH)
    used = jnp.where(groups == busiest, PAIR_CAP, used)
    first_local = jax.random.randint(split_keys[2], (group_count, PAIR_CAP), 0, IMG_DEV)
    first_local = jnp.where(slot_ids[None, :] < IMG_DEV, slot_ids[None, :], first_local)
    ahead = jax.random.randint(split_keys[3], (group_count, PAIR_CAP), 0, REACH + 1)
    ahead = jnp.where((groups[:, None] == busiest) & (slot_ids[None, :] == 0), REACH, ahead)
    ahead = jnp.minimum(ahead, group_count - 1 - groups[:, None])
    second_local = jax.random.randint(split_keys[4], (group_count, PAIR_CAP), 0, IMG_DEV)
    first_image = groups[:, None] * IMG_DEV + first_local
    second_image = (groups[:, None] + ahead) * IMG_DEV + second_local
    second_image = jnp.where(second_image == first_image, groups[:, None] * IMG_DEV + (first_local + 1) % IMG_DEV, second_image)
    live = slot_ids[None, :] < used[:, None]
    result = jnp.stack([jnp.where(live, first_image, -1), jnp.where(live, second_image, -1)], axis=-1)
    return result.reshape(PAIRS, 2).astype(jnp.int32)


def scatter_about(rng, extent, scale, bound, dtype=jnp.bfloat16):
    values = scale * jax.random.normal(rng, extent, jnp.float32)
    return jnp.clip(values, min=-bound, max=bound).astype(dtype)


def setup_inputs(seed: int = 0, part: int = 0) -> dict:
    streams_of = jax.random.split(jax.random.key(seed), 10)
    part_splits = jax.random.split(jax.random.fold_in(streams_of[9], part), 10)
    return {
        "descriptors": draw_descriptors(jax.random.fold_in(jax.random.fold_in(streams_of[9], part), 71), part),
        "pair_list": draw_pair_list(jax.random.fold_in(jax.random.fold_in(streams_of[9], part), 71), part),
        "key_proj": scatter_about(streams_of[2], (D, D), D ** -0.5, 0.375),
        "value_proj": scatter_about(streams_of[3], (D, D), D ** -0.5, 0.375),
        "out_proj": scatter_about(streams_of[4], (D, D), D ** -0.5, 0.375),
        "ffn_first": scatter_about(streams_of[5], (HID, HID), HID ** -0.5, 0.25),
        "norm_gain": jnp.clip(1.0 + 0.1 * jax.random.normal(streams_of[6], (HID,), jnp.float32), 0.5, 1.5),
        "norm_bias": scatter_about(streams_of[7], (HID,), 0.5, 3.0, jnp.float32),
        "ffn_second": scatter_about(streams_of[8], (HID, D), HID ** -0.5, 0.25),
    }


EMPTY_MAX = -1e+29

def rounded(values):
    return lax.optimization_barrier(values.astype(jnp.bfloat16)).astype(jnp.float32)

def product(left_side, right_side):
    return jnp.dot(left_side.astype(jnp.float32), right_side.astype(jnp.float32), precision=lax.Precision.HIGHEST)

def pair_pieces(first_keys, first_values, second_keys, second_values):
    head_size = D // HEADS
    score_scale = 1.0 / math.sqrt(head_size)
    row_maxima, row_totals, row_sums = ([], [], [])
    col_maxima, col_totals, col_sums = ([], [], [])
    for h in range(HEADS):
        low_col = h * head_size
        high_col = low_col + head_size
        scores = product(first_keys[:, low_col:high_col], second_keys[:, low_col:high_col].T) * score_scale
        row_max = lax.optimization_barrier(jnp.max(scores, axis=1))
        row_weights = jnp.exp(scores - row_max[:, None])
        row_maxima.append(row_max)
        row_totals.append(lax.optimization_barrier(jnp.sum(row_weights, axis=1)))
        row_sums.append(product(rounded(row_weights), second_values[:, low_col:high_col]))
        col_max = lax.optimization_barrier(jnp.max(scores, axis=0))
        col_weights = jnp.exp(scores - col_max[None, :])
        col_maxima.append(col_max)
        col_totals.append(lax.optimization_barrier(jnp.sum(col_weights, axis=0)))
        col_sums.append(product(rounded(col_weights).T, first_values[:, low_col:high_col]))
    return (jnp.stack(row_maxima), jnp.stack(row_totals), jnp.concatenate(row_sums, axis=1), jnp.stack(col_maxima), jnp.stack(col_totals), jnp.concatenate(col_sums, axis=1))

def scaled_sums(numbers, factors):
    points = numbers.shape[-2]
    shaped = numbers.reshape(numbers.shape[:-2] + (points, HEADS, D // HEADS))
    return (shaped * jnp.swapaxes(factors, -1, -2)[..., None]).reshape(numbers.shape)

def combine(earlier, later):
    early_max, early_den, early_num = earlier
    late_max, late_den, late_num = later
    top_max = jnp.maximum(early_max, late_max)
    early_factor = jnp.exp(early_max - top_max)
    late_factor = jnp.exp(late_max - top_max)
    total_den = early_factor * early_den + late_factor * late_den
    total_num = scaled_sums(early_num, early_factor) + scaled_sums(late_num, late_factor)
    return (top_max, total_den, total_num)

def finish_layer(flat_rows, totals, out_proj, ffn_first, norm_gain, norm_bias, ffn_second):
    maxima, denoms, numers = totals
    images, points, features = numers.shape
    message = numers.reshape(images, points, HEADS, features // HEADS) / jnp.swapaxes(denoms, 1, 2)[..., None]
    message = rounded(message.reshape(images * points, features))
    told = rounded(product(message, out_proj))
    joined = jnp.concatenate([flat_rows.astype(jnp.float32), told], axis=1)
    hidden = product(joined, ffn_first)
    centre = lax.optimization_barrier(jnp.mean(hidden, axis=1, keepdims=True))
    deviation = hidden - centre
    second_moment = lax.optimization_barrier(jnp.mean(deviation * deviation, axis=1, keepdims=True))
    normed = deviation * lax.rsqrt(second_moment + 1e-05) * norm_gain + norm_bias
    active = rounded(jax.nn.gelu(normed, approximate=False))
    return (flat_rows.astype(jnp.float32) + product(active, ffn_second)).astype(jnp.bfloat16)

def reference(descriptors, pair_list, key_proj, value_proj, out_proj, ffn_first, norm_gain, norm_bias, ffn_second):
    images, points, features = descriptors.shape
    flat_rows = descriptors.reshape(images * points, features)
    keys_all = rounded(product(flat_rows, key_proj)).reshape(images, points, features)
    values_all = rounded(product(flat_rows, value_proj)).reshape(images, points, features)
    start = (jnp.full((images, HEADS, points), EMPTY_MAX, jnp.float32), jnp.zeros((images, HEADS, points), jnp.float32), jnp.zeros((images, points, features), jnp.float32))

    def fold_image(totals, image, pieces):
        current = tuple((lax.dynamic_index_in_dim(item, image, 0) for item in totals))
        merged = combine(current, tuple((piece[None] for piece in pieces)))
        return tuple((lax.dynamic_update_index_in_dim(item, new_item, image, 0) for item, new_item in zip(totals, merged)))

    def visit(totals, pair_row):

        def work(running):
            first_image = pair_row[0]
            second_image = pair_row[1]
            pieces = pair_pieces(keys_all[first_image], values_all[first_image], keys_all[second_image], values_all[second_image])
            running = fold_image(running, first_image, pieces[:3])
            return fold_image(running, second_image, pieces[3:])

        def keep(running):
            return running
        return (lax.cond(pair_row[0] >= 0, work, keep, totals), None)
    totals, _ = lax.scan(visit, start, pair_list)
    result = finish_layer(flat_rows, totals, out_proj, ffn_first, norm_gain, norm_bias, ffn_second)
    return result.reshape(images, points, features)
```

```python
import functools
import math

import jax
import jax.numpy as jnp
from jax import lax
from jax.experimental import pallas as pl
from jax.experimental.pallas import tpu as pltpu
from jax.sharding import PartitionSpec as P

HEADS = 4
REACH = 2
LANES = 128
EXTRA = 16
EMPTY_MAX = -1e29
LOG2E = math.log2(math.e)
DEN_LOW, DEN_HIGH = 2.0**-80, 2.0**100

f32, bf16, i32 = jnp.float32, jnp.bfloat16, jnp.int32
PLAIN = (((1,), (0,)), ((), ()))
TRANS = (((1,), (1,)), ((), ()))

OWN, SWAP, SHARED, REST, RELAY = range(5)
SLOT_OFFSETS = ((0, 1, 2, -2, -1), (0, -1, -2, 2, 1))


def dot(left, right, dims=PLAIN):
    return lax.dot_general(left, right, dims, preferred_element_type=f32)


class Shape:
    def __init__(self, images, points, features, slots):
        self.images, self.points, self.features, self.slots = images, points, features, slots
        self.head = features // HEADS
        self.per_block = LANES // self.head
        self.blocks = HEADS // self.per_block
        self.acc_rows = self.head + 16
        self.rows = images * points
        self.packed = self.rows + EXTRA
        self.window = images * (REACH + 1)
        self.radix = images * self.window + 1
        self.limit = 2 * slots * (REACH + 1)

    def head_at(self, h):
        block, i = divmod(h, self.per_block)
        return block, i, slice(i * self.points, (i + 1) * self.points)


def pack_rows(descriptors, pair_list, sh):
    local = pair_list - lax.axis_index("img") * sh.images
    codes = jnp.where(pair_list[:, 0] >= 0, 1 + local[:, 0] * sh.window + local[:, 1], 0)
    tail = jnp.pad(codes.astype(bf16)[None, :], ((0, EXTRA - 1), (0, sh.features - sh.slots)))
    return jnp.concatenate([descriptors.reshape(sh.rows, sh.features), tail], axis=0)


def own_digits(pair_ref, sh, base):
    return [(pair_ref[r, 0] >= 0, pair_ref[r, 0] - base, pair_ref[r, 1] - base) for r in range(sh.slots)]


def tail_digits(tail, sh):
    lane = lax.broadcasted_iota(i32, tail.shape, 1)
    weight = jnp.zeros(tail.shape, f32)
    for r in range(sh.slots):
        weight = jnp.where(lane == r, float(sh.radix**r), weight)
    total = jnp.sum(tail.astype(f32) * weight).astype(i32)
    out = []
    for r in range(sh.slots):
        code = lax.rem(lax.div(total, i32(sh.radix**r)), i32(sh.radix))
        spot = jnp.maximum(code - 1, 0)
        out.append((code > 0, lax.div(spot, i32(sh.window)), lax.rem(spot, i32(sh.window))))
    return out


def add_tasks(tasks, count, sh, slot, odd, own, theirs):
    offset = jnp.where(odd, SLOT_OFFSETS[1][slot], SLOT_OFFSETS[0][slot])
    images = i32(sh.images)

    def push(count, ok, query, source):
        @pl.when(ok)
        def _():
            tasks[3 * count] = query
            tasks[3 * count + 1] = slot
            tasks[3 * count + 2] = source

        return count + ok.astype(i32)

    for used, first, second in own:
        ok = jnp.logical_and(used, lax.div(second, images) == offset)
        count = push(count, ok, first, lax.rem(second, images))
    for used, first, second in theirs:
        ok = jnp.logical_and(used, lax.div(second, images) == -offset)
        count = push(count, ok, lax.rem(second, images), first)
    return count


def source_rows(win, slot, image, sh):
    return win[slot, pl.ds(pl.multiple_of(image * sh.points, 16), sh.points), :]


def project_source(rows, wk_ref, wv_t, vx, sh):
    k = dot(rows, wk_ref[...]).astype(bf16)
    vt = dot(wv_t[...], rows, TRANS).astype(bf16)
    for h in range(HEADS):
        vx[h, : sh.head, :] = vt[h * sh.head : (h + 1) * sh.head, :]
    return k


def plain_task(query, rows, wk_ref, wv_t, qt, vx, acc, sh):
    k = project_source(rows, wk_ref, wv_t, vx, sh)
    for block in range(sh.blocks):
        scores = dot(k[:, block * LANES : (block + 1) * LANES], qt[query, block])
        weights = jnp.exp2(scores).astype(bf16)
        for i in range(sh.per_block):
            h = block * sh.per_block + i
            acc[query, h] = acc[query, h] + dot(vx[h], weights[:, i * sh.points : (i + 1) * sh.points])


def shifted_task(query, rows, wk_ref, wv_t, qt, vx, acc, top, sh):
    k = project_source(rows, wk_ref, wv_t, vx, sh)
    for h in range(HEADS):
        block, _, cols = sh.head_at(h)
        scores = dot(k[:, block * LANES : (block + 1) * LANES], qt[query, block, :, cols])
        old = top[query, h]
        new = jnp.maximum(old, jnp.max(scores, axis=0, keepdims=True))
        weights = jnp.exp2(scores - new).astype(bf16)
        top[query, h] = new
        acc[query, h] = acc[query, h] * jnp.exp2(old - new) + dot(vx[h], weights)


def run_tasks(tasks, count, task, win, sh):
    def body(t, carry):
        task(tasks[3 * t], source_rows(win, tasks[3 * t + 1], tasks[3 * t + 2], sh))
        return carry

    lax.fori_loop(0, count, body, 0)


def fetches(refs, win, sems, slots):
    return [pltpu.make_async_copy(refs[s], win.at[s], sems.at[s]) for s in slots]


def start(copies):
    for copy in copies:
        copy.start()


def wait(copies):
    for copy in copies:
        copy.wait()


def place(sh):
    group = lax.axis_index("img")
    return lax.rem(group, 2) == 1, group * sh.images


def tail_of(win, slot, sh):
    return tail_digits(win[slot, sh.rows : sh.rows + EXTRA, :LANES], sh)


def local_kernel(sh, pair_ref, own_ref, swap_ref, wk_ref, wv_ref, acc, qt, win, wv_t, vx, tasks, sems):
    copies = fetches((own_ref, swap_ref), win, sems, (OWN, SWAP))
    start(copies)
    odd, base = place(sh)
    acc[...] = jnp.zeros_like(acc)
    qt[...] = jnp.zeros_like(qt)
    vx[...] = jnp.ones_like(vx)
    wk_t = wk_ref[...].T
    wv_t[...] = wv_ref[...].T
    wait(copies)
    for n in range(sh.images):
        rows = win[OWN, n * sh.points : (n + 1) * sh.points, :]
        q = (dot(wk_t, rows, TRANS) * (LOG2E / math.sqrt(sh.head))).astype(bf16)
        for h in range(HEADS):
            block, i, cols = sh.head_at(h)
            qt[n, block, i * sh.head : (i + 1) * sh.head, cols] = q[h * sh.head : (h + 1) * sh.head, :]
    own = own_digits(pair_ref, sh, base)
    count = add_tasks(tasks, i32(0), sh, OWN, odd, own, own)
    count = add_tasks(tasks, count, sh, SWAP, odd, own, tail_of(win, SWAP, sh))
    run_tasks(tasks, count, lambda q, rows: plain_task(q, rows, wk_ref, wv_t, qt, vx, acc, sh), win, sh)


def shared_kernel(sh, pair_ref, shared_ref, wk_ref, wv_ref, qt, acc_in, acc, win, wv_t, vx, tasks, sems):
    copies = [pltpu.make_async_copy(shared_ref, win.at[SHARED], sems.at[0])]
    start(copies)
    odd, base = place(sh)
    acc[...] = acc_in[...]
    vx[...] = jnp.ones_like(vx)
    wv_t[...] = wv_ref[...].T
    wait(copies)
    own = own_digits(pair_ref, sh, base)
    count = add_tasks(tasks, i32(0), sh, SHARED, odd, own, tail_of(win, SHARED, sh))
    run_tasks(tasks, count, lambda q, rows: plain_task(q, rows, wk_ref, wv_t, qt, vx, acc, sh), win, sh)


def last_kernel(
    sh, pair_ref, own_ref, swap_ref, shared_ref, rest_ref, relay_ref, wk_ref, wv_ref, qt, acc_in,
    out_proj, ffn_first, gain, bias, ffn_second, result, acc, top, win, wv_t, vx, tasks, sems,
):
    refs = (own_ref, swap_ref, shared_ref, rest_ref, relay_ref)
    copies = fetches(refs, win, sems, (RELAY, REST, OWN))
    start(copies)
    odd, base = place(sh)
    acc[...] = acc_in[...]
    vx[...] = jnp.ones_like(vx)
    wv_t[...] = wv_ref[...].T
    wait(copies)
    own = own_digits(pair_ref, sh, base)
    count = add_tasks(tasks, i32(0), sh, RELAY, odd, own, tail_of(win, RELAY, sh))
    count = add_tasks(tasks, count, sh, REST, odd, own, tail_of(win, REST, sh))
    run_tasks(tasks, count, lambda q, rows: plain_task(q, rows, wk_ref, wv_t, qt, vx, acc, sh), win, sh)

    dens = acc[:, :, sh.head, :]
    fine = jnp.logical_and(jnp.min(dens) >= DEN_LOW, jnp.max(dens) <= DEN_HIGH)

    @pl.when(jnp.logical_not(fine))
    def _():
        more = fetches(refs, win, sems, (SWAP, SHARED))
        start(more)
        wait(more)
        acc[...] = jnp.zeros_like(acc)
        top[...] = jnp.full_like(top, EMPTY_MAX)
        count = add_tasks(tasks, i32(0), sh, OWN, odd, own, own)
        for slot in (SWAP, SHARED, REST, RELAY):
            count = add_tasks(tasks, count, sh, slot, odd, own, tail_of(win, slot, sh))
        task = lambda q, rows: shifted_task(q, rows, wk_ref, wv_t, qt, vx, acc, top, sh)
        run_tasks(tasks, count, task, win, sh)

    def finish(n, carry):
        parts = [acc[n, h, : sh.head, :] / acc[n, h, sh.head : sh.head + 1, :] for h in range(HEADS)]
        message = jnp.concatenate(parts, axis=0).T.astype(bf16)
        rows = source_rows(win, OWN, n, sh)
        told = dot(message, out_proj[...]).astype(bf16)
        hidden = dot(rows, ffn_first[: sh.features, :]) + dot(told, ffn_first[sh.features :, :])
        deviation = hidden - jnp.mean(hidden, axis=1, keepdims=True)
        second = jnp.mean(deviation * deviation, axis=1, keepdims=True)
        normed = deviation * lax.rsqrt(second + 1e-05) * gain[...] + bias[...]
        active = (0.5 * normed * (1.0 + lax.erf(normed * math.sqrt(0.5)))).astype(bf16)
        result[n] = (rows.astype(f32) + dot(active, ffn_second[...])).astype(bf16)
        return carry

    lax.fori_loop(0, sh.images, finish, 0)


SMEM = pl.BlockSpec(memory_space=pltpu.SMEM)
VMEM = pl.BlockSpec(memory_space=pltpu.VMEM)
ANY = pl.BlockSpec(memory_space=pl.ANY)


def shards(
    descriptors, pair_list, key_proj, value_proj, out_proj, ffn_first, norm_gain, norm_bias, ffn_second
):
    images, points, features = descriptors.shape
    sh = Shape(images, points, features, pair_list.shape[0])
    devices = lax.axis_size("img")

    def send(block, routes):
        return lax.ppermute(block, "img", [(a, b) for a, b in routes if 0 <= a < devices and 0 <= b < devices])

    pairs = range(0, devices, 2)
    partner = [(i, i ^ 1) for i in range(devices)]
    packed = pack_rows(descriptors, pair_list, sh)
    shared = send(packed, [(c + 2, c) for c in pairs] + [(c - 1, c + 1) for c in pairs])
    swap = send(packed, partner)
    rest = send(packed, [(c - 2, c) for c in pairs] + [(c + 3, c + 1) for c in pairs])
    relay = send(shared, partner)

    acc_shape = (images, HEADS, sh.acc_rows, points)
    qt_shape = (images, sh.blocks, LANES, sh.per_block * points)
    common = [
        pltpu.VMEM((features, features), bf16),
        pltpu.VMEM((HEADS, sh.acc_rows, points), bf16),
        pltpu.SMEM((3 * sh.limit,), i32),
        pltpu.SemaphoreType.DMA((5,)),
    ]
    task_flops = 2 * points * features * 2 * features + 4 * points * points * features

    def cost(task_count, extra=0):
        return pl.CostEstimate(
            flops=task_count * task_flops + extra, bytes_accessed=4 << 20, transcendentals=task_count * HEADS * points**2
        )

    def params():
        return pltpu.CompilerParams(vmem_limit_bytes=48 << 20)

    acc, qt = pl.pallas_call(
        functools.partial(local_kernel, sh),
        out_shape=(jax.ShapeDtypeStruct(acc_shape, f32), jax.ShapeDtypeStruct(qt_shape, bf16)),
        in_specs=[SMEM, ANY, ANY, VMEM, VMEM],
        out_specs=(VMEM, VMEM),
        scratch_shapes=[pltpu.VMEM((2, sh.packed, features), bf16), *common],
        cost_estimate=cost(4),
        compiler_params=params(),
        name="local_parts",
    )(pair_list, packed, swap, key_proj, value_proj)
    acc = pl.pallas_call(
        functools.partial(shared_kernel, sh),
        out_shape=jax.ShapeDtypeStruct(acc_shape, f32),
        in_specs=[SMEM, ANY, VMEM, VMEM, VMEM, VMEM],
        out_specs=VMEM,
        scratch_shapes=[pltpu.VMEM((3, sh.packed, features), bf16), *common],
        cost_estimate=cost(2),
        compiler_params=params(),
        name="shared_parts",
    )(pair_list, shared, key_proj, value_proj, qt, acc)
    return pl.pallas_call(
        functools.partial(last_kernel, sh),
        out_shape=jax.ShapeDtypeStruct(descriptors.shape, bf16),
        in_specs=[SMEM, ANY, ANY, ANY, ANY, ANY, *[VMEM] * 9],
        out_specs=VMEM,
        scratch_shapes=[
            pltpu.VMEM(acc_shape, f32),
            pltpu.VMEM((images, HEADS, 1, points), f32),
            pltpu.VMEM((5, sh.packed, features), bf16),
            *common,
        ],
        cost_estimate=cost(4),
        compiler_params=params(),
        name="last_parts",
    )(
        pair_list, packed, swap, shared, rest, relay, key_proj, value_proj, qt, acc,
        out_proj, ffn_first, norm_gain[None, :], norm_bias[None, :], ffn_second,
    )


def solution(mesh):
    per_device = P(("groups", "img"))
    in_specs = (per_device, per_device, *[P()] * 7)
    return jax.shard_map(shards, mesh=mesh, in_specs=in_specs, out_specs=per_device, check_vma=False)
```
